32 devices in a mesh: img: 2 (over core), band: 4 (over z), pw: 4 (over y, x).
Axes of the slice: x: 2, y: 2, z: 4, core: 2. Of those that a mesh axis runs over, the one named last changes fastest.
Arguments:
- coefficients: bfloat16 [2, 1024, 32, 2048], P('img', None, ('band', 'pw')), may hold values from -6 to 6
- rotation: bfloat16 [2, 1024, 256], P('img'), may hold values from -0.1875 to 0.1875
- positions: int32 [2, 3, 256], P('img'), may hold values from 0 to 63, as said below
- start_pos: int32 [3, 256], replicated, may hold values from 0 to 63, as said below
- end_pos: int32 [3, 256], replicated, may hold values from 0 to 63, as said below
- species: int32 [256], replicated, may hold values from 0 to 3
- depth: float32 [4], replicated, may hold values from 0.5 to 3
Outputs:
- correction: bfloat16 [2, 256, 32, 2048], P('img', None, ('band', 'pw'))
- ritz_values: float32 [2, 256], P('img')
- band_force: float32 [2, 3, 256], P('img')
- along_force: float32 [2], P('img')
The draws below stay inside these ranges and needn't reach their ends.
Inputs may be any that keep to these rules, and one draw needn't show every extreme that they name: `positions`: grid index of each atom's centre along each dimension. `start_pos`: grid index of each atom's centre along each dimension. `end_pos`: grid index of each atom's centre along each dimension.
All inputs are finite; a program needn't handle non-finite values.
Results may differ from the reference program's by a relative error of at most 0.012.
The reference program's roundings to bfloat16 on the way count: a program that leaves them out, or rounds other values in their place, can miss the bound.
Values may be sent and summed in bfloat16 or wider, within the bound.
A program may use at most 128 MiB of HBM per device.

```python
import math
import jax
import jax.numpy as jnp
from jax import lax

G = 64
W = 32
BANDS = 1024
BLOCK = 256
ATOMS = 256
SPECIES = 4
IMAGES = 2
NPW = 32768


def common_base(key):
    return jax.random.randint(jax.random.fold_in(key, 11), (3, ATOMS), 0, G)


def displaced(key, salt_value, shape_full):
    return jax.random.randint(jax.random.fold_in(key, salt_value), shape_full, -2, 3)


def draw_positions(key, part):
    base_grid = common_base(key)
    return jnp.mod(base_grid[None] + displaced(key, 12, (IMAGES, 3, ATOMS)), G).astype(jnp.int32)


def draw_start_pos(key, part):
    base_grid = common_base(key)
    return jnp.mod(base_grid + displaced(key, 13, (3, ATOMS)), G).astype(jnp.int32)


def draw_end_pos(key, part):
    base_grid = common_base(key)
    return jnp.mod(base_grid + displaced(key, 14, (3, ATOMS)), G).astype(jnp.int32)


def with_ends(values, stream_key, least, high):
    index_at = [jax.random.randint(jax.random.fold_in(stream_key, axis), (), 0, length) for axis, length in enumerate(values.shape)]
    main_axis = values.shape.index(max(values.shape))
    next_to = index_at[:main_axis] + [(index_at[main_axis] + 1) % values.shape[main_axis]] + index_at[main_axis + 1:]
    return values.at[tuple(index_at)].set(least).at[tuple(next_to)].set(high)


def levels(own_key, shape, pieces, smallest, largest):
    level = 1.0
    for axis_at, shards_of in pieces:
        steps = jax.random.uniform(jax.random.fold_in(jax.random.fold_in(own_key, 6), axis_at), (shards_of,), jnp.float32, smallest / len(pieces), largest / len(pieces))
        level = level * jnp.repeat(jnp.exp(steps), shape[axis_at] // shards_of).reshape((-1,) + (1,) * (len(shape) - 1 - axis_at))
    return level


def normal_values(own_key, shape, scale, reach, pieces=(), held_as=jnp.bfloat16):
    drawn = jax.random.normal(own_key, shape, jnp.float32) * scale
    if len(pieces) > 0:
        drawn = levels(own_key, shape, pieces, -0.22, 0.18) * drawn
    return jnp.clip(drawn, min=-reach, max=reach).astype(held_as)


def setup_inputs(seed: int = 0) -> dict:
    splits = jax.random.split(jax.random.key(seed), 8)
    return {
        "coefficients": normal_values(splits[0], (IMAGES, BANDS, W, W * 2 * W), 1.0, 6.0, ((0, 2), (2, 16))),
        "rotation": normal_values(splits[1], (IMAGES, BANDS, BLOCK), BANDS ** -0.5, 0.1875, ((0, 2),)),
        "positions": draw_positions(jax.random.fold_in(splits[7], 71), 0),
        "start_pos": draw_start_pos(jax.random.fold_in(splits[7], 71), 0),
        "end_pos": draw_end_pos(jax.random.fold_in(splits[7], 71), 0),
        "species": with_ends(jax.random.randint(splits[5], (ATOMS,), 0, SPECIES), jax.random.fold_in(splits[5], 1), 0, SPECIES - 1).astype(jnp.int32),
        "depth": jnp.clip(jnp.exp(jax.random.uniform(splits[6], (SPECIES,), jnp.float32, math.log(0.5), math.log(3.0))), 0.5, 3.0),
    }


kinetic_scale = 0.01
sigma_cells = 3.0
spring_constant = 2.0
epsilon = 1e-06
highest = lax.Precision.HIGHEST

def product(pattern, left_op, right_op):
    return jnp.einsum(pattern, left_op.astype(jnp.float32), right_op.astype(jnp.float32), precision=highest)

def phases(box_order, box_size, grid_size):
    wavenum = box_order.astype(jnp.int32) - box_size // 2
    grid_cells = jnp.arange(grid_size, dtype=jnp.int32)
    turn_count = jnp.mod(wavenum[:, None] * grid_cells[None, :], grid_size)
    return turn_count.astype(jnp.float32) * (2.0 * math.pi / grid_size)

def forward_table(box_order, box_size, grid_size):
    angle_tab = phases(box_order, box_size, grid_size)
    cosine = jnp.cos(angle_tab) / math.sqrt(box_size)
    sine_part = jnp.sin(angle_tab) / math.sqrt(box_size)
    dft_table = jnp.stack([jnp.stack([cosine, sine_part], 1), jnp.stack([-sine_part, cosine], 1)], 0)
    return dft_table.astype(jnp.bfloat16)

def inverse_table(box_order, box_size, grid_size):
    angle_tab = phases(box_order, box_size, grid_size).T
    factor = math.sqrt(box_size) / grid_size
    cosine = jnp.cos(angle_tab) * factor
    sine_part = jnp.sin(angle_tab) * factor
    dft_table = jnp.stack([jnp.stack([cosine, -sine_part], 1), jnp.stack([sine_part, cosine], 1)], 0)
    return dft_table.astype(jnp.bfloat16)

def section_zy(coeff_block, table_z, table_y):
    leading = coeff_block.shape[0]
    planes = coeff_block.shape[1]
    split_up = coeff_block.reshape(leading, planes, W, 2, W)
    along_z = product('blyck,ckdn->blydn', split_up, table_z).astype(jnp.bfloat16)
    along_y = product('blycz,cydm->blmdz', along_z, table_y).astype(jnp.bfloat16)
    return along_y.reshape(leading, planes, G * 2 * G)

def section_x(arrived, table_x):
    leading = arrived.shape[0]
    y_rows = arrived.shape[2] // (2 * G)
    split_up = arrived.reshape(leading, W, y_rows, 2, G)
    return product('bxycz,cxdn->bnydz', split_up, table_x)

def section_x_inverse(weighted, table_x):
    leading = weighted.shape[0]
    y_rows = weighted.shape[2]
    along_x = product('bnydz,dncx->bxycz', weighted, table_x).astype(jnp.bfloat16)
    return along_x.reshape(leading, W, y_rows * 2 * G)

def section_zy_inverse(returned, table_y, table_z):
    leading = returned.shape[0]
    planes = returned.shape[1]
    split_up = returned.reshape(leading, planes, G, 2, G)
    along_y = product('blmdz,dmcy->blycz', split_up, table_y).astype(jnp.bfloat16)
    along_z = product('blydn,dnck->blyck', along_y, table_z)
    return along_z.reshape(leading, planes, W * 2 * W)

def wrap_offset(values):
    return jnp.mod(values + G // 2, G) - G // 2

def gaussians(coords, grid_cells):
    offset = wrap_offset(grid_cells[None, :] - coords[:, None]).astype(jnp.float32)
    return (jnp.exp(-offset * offset / (2.0 * sigma_cells * sigma_cells)), offset)

def atom_tables(own_pos, y_cells):
    grid_cells = jnp.arange(G, dtype=jnp.int32)
    gauss_x, offset_x = gaussians(own_pos[0], grid_cells)
    gauss_y, offset_y = gaussians(own_pos[1], y_cells)
    gauss_z, offset_z = gaussians(own_pos[2], grid_cells)
    return (gauss_x, offset_x, gauss_y, offset_y, gauss_z, offset_z)

def local_potential(tables, strength):
    gauss_x, offset_x, gauss_y, offset_y, gauss_z, offset_z = tables
    atom_count = gauss_x.shape[0]
    joined = (gauss_y[:, :, None] * gauss_z[:, None, :]).reshape(atom_count, -1)
    potential = jnp.dot((strength[:, None] * gauss_x).T, joined, precision=highest)
    return (potential, joined)

def atom_forces(density, tables, joined, strength):
    gauss_x, offset_x, gauss_y, offset_y, gauss_z, offset_z = tables
    atom_count = gauss_x.shape[0]
    with_y = ((gauss_y * offset_y)[:, :, None] * gauss_z[:, None, :]).reshape(atom_count, -1)
    with_z = (gauss_y[:, :, None] * (gauss_z * offset_z)[:, None, :]).reshape(atom_count, -1)
    stacked = jnp.concatenate([joined, with_y, with_z], 0)
    moments = jnp.dot(density, stacked.T, precision=highest)
    prefactor = -strength / (sigma_cells * sigma_cells)
    force_x = prefactor * lax.optimization_barrier(jnp.sum(gauss_x * offset_x * moments[:, :atom_count].T, 1))
    force_y = prefactor * lax.optimization_barrier(jnp.sum(gauss_x * moments[:, atom_count:2 * atom_count].T, 1))
    force_z = prefactor * lax.optimization_barrier(jnp.sum(gauss_x * moments[:, 2 * atom_count:].T, 1))
    return jnp.stack([force_x, force_y, force_z], 0)

def kinetic_table(x_cells):
    entries = jnp.arange(W * 2 * W, dtype=jnp.int32)
    wave_y = entries // (2 * W) - W // 2
    wave_z = jnp.mod(entries, W) - W // 2
    wave_x = x_cells - W // 2
    squared = wave_x[:, None] * wave_x[:, None] + (wave_y * wave_y + wave_z * wave_z)[None, :]
    return kinetic_scale * 0.5 * squared.astype(jnp.float32)

def rotate_quarter(values):
    leading = values.shape[0]
    middle = values.shape[1]
    split_up = values.reshape(leading, middle, W, 2, W)
    turned = jnp.stack([-split_up[:, :, :, 1, :], split_up[:, :, :, 0, :]], 3)
    return turned.reshape(values.shape)

def chain_forces(force, own_pos, before, after):
    ahead_step = wrap_offset(after - own_pos).astype(jnp.float32)
    behind = wrap_offset(own_pos - before).astype(jnp.float32)
    tangent_raw = ahead_step + behind
    entries = 3 * own_pos.shape[1]
    tangent = tangent_raw * lax.rsqrt(jnp.mean(tangent_raw * tangent_raw) + epsilon) / math.sqrt(entries)
    length_ahead = jnp.sqrt(entries * (jnp.mean(ahead_step * ahead_step) + epsilon))
    length_behind = jnp.sqrt(entries * (jnp.mean(behind * behind) + epsilon))
    along_path = jnp.sum(force * tangent)
    band_push = force - along_path * tangent + spring_constant * (length_ahead - length_behind) * tangent
    return (band_push, along_path)

def one_image(coeffs, rotation_one, own_pos, before, after, strength):
    flat_all = coeffs.reshape(BANDS, -1)
    orbitals = jnp.dot(rotation_one.T, flat_all, preferred_element_type=jnp.float32).astype(jnp.bfloat16)
    orbitals = orbitals.reshape(BLOCK, W, W * 2 * W)
    natural = jnp.arange(W, dtype=jnp.int32)
    table_f = forward_table(natural, W, G)
    table_i = inverse_table(natural, W, G)
    tables = atom_tables(own_pos, jnp.arange(G, dtype=jnp.int32))
    potential, joined = local_potential(tables, strength)
    grid_potential = potential.reshape(G, G, G)
    group_size = math.gcd(BLOCK, 16)
    blocks = orbitals.reshape(BLOCK // group_size, group_size, W, W * 2 * W)

    def apply_block(density, band_block):
        spread = section_zy(band_block, table_f, table_f)
        in_space = section_x(spread, table_f)
        density = density + lax.optimization_barrier(jnp.sum(in_space * in_space, axis=(0, 3)))
        weighted = (in_space * grid_potential[:, :, None, :]).astype(jnp.bfloat16)
        returned = section_x_inverse(weighted, table_i)
        return (density, section_zy_inverse(returned, table_i, table_i))
    density, applied = lax.scan(apply_block, jnp.zeros((G, G, G), jnp.float32), blocks)
    applied = applied.reshape(BLOCK, W, W * 2 * W)
    kinetic = kinetic_table(natural)
    orbitals_wide = orbitals.astype(jnp.float32)
    hamiltonian = kinetic[None] * orbitals_wide + applied
    numerator = lax.optimization_barrier(jnp.sum(orbitals_wide * hamiltonian, axis=(1, 2)))
    denominator = lax.optimization_barrier(jnp.sum(orbitals_wide * orbitals_wide, axis=(1, 2)))
    ritz_values = numerator / NPW / (denominator / NPW + epsilon)
    residual = hamiltonian - ritz_values[:, None, None] * orbitals_wide
    search = (residual / (1.0 + kinetic)[None]).astype(jnp.bfloat16)
    search_pair = jnp.concatenate([search.reshape(BLOCK, -1), (-rotate_quarter(search)).reshape(BLOCK, -1)], 0)
    intersections = jnp.dot(flat_all, search_pair.T, preferred_element_type=jnp.float32) / NPW
    intersections = intersections.astype(jnp.bfloat16)
    projected = jnp.dot(intersections.T, flat_all, preferred_element_type=jnp.float32)
    projection = projected[:BLOCK].reshape(BLOCK, W, -1) + rotate_quarter(projected[BLOCK:].reshape(BLOCK, W, -1))
    correction = (search.astype(jnp.float32) - projection).astype(jnp.bfloat16)
    atom_force = atom_forces((density / BLOCK).reshape(G, G * G), tables, joined, strength)
    band_push, along_path = chain_forces(atom_force, own_pos, before, after)
    return (correction, ritz_values, band_push, along_path)

def reference(coefficients, rotation, positions, start_pos, end_pos, species, depth):
    kind_ids = jnp.arange(SPECIES, dtype=jnp.int32)
    strength = lax.optimization_barrier(jnp.sum(jnp.where(species[:, None] == kind_ids[None, :], depth[None, :], 0.0), 1))
    results = []
    for image_idx in range(IMAGES):
        before = start_pos if image_idx == 0 else positions[image_idx - 1]
        after = end_pos if image_idx == IMAGES - 1 else positions[image_idx + 1]
        results.append(one_image(coefficients[image_idx], rotation[image_idx], positions[image_idx], before, after, strength))
    return (jnp.stack([entry_one[0] for entry_one in results], 0), jnp.stack([entry_one[1] for entry_one in results], 0), jnp.stack([entry_one[2] for entry_one in results], 0), jnp.stack([entry_one[3] for entry_one in results], 0))
```

```python
import math

import jax
import jax.numpy as jnp
import numpy as np
from jax import lax
from jax.experimental import pallas as pl
from jax.experimental.pallas import tpu as pltpu
from jax.sharding import PartitionSpec as P

G = 64
W = 32
BANDS = 1024
BLOCK = 256
SPECIES = 4


kinetic_scale = 0.01
sigma_cells = 3.0
spring_constant = 2.0
epsilon = 1e-06
highest = lax.Precision.HIGHEST


def passed_along(block, axis, distance):
    devices = range(lax.axis_size(axis))
    route = [(i - distance, i) for i in devices if i - distance in devices]
    return lax.ppermute(block, axis, route)


def phases():
    wavenum = np.arange(W, dtype=np.int32) - W // 2
    grid_cells = np.arange(G, dtype=np.int32)
    turn_count = np.mod(wavenum[:, None] * grid_cells[None, :], G)
    return turn_count.astype(np.float32) * np.float32(2.0 * math.pi / G)


def forward_table():
    angle_tab = phases()
    cosine = np.cos(angle_tab) / np.float32(math.sqrt(W))
    sine_part = np.sin(angle_tab) / np.float32(math.sqrt(W))
    return np.stack([np.stack([cosine, sine_part], 1), np.stack([-sine_part, cosine], 1)], 0)


def inverse_table():
    angle_tab = phases().T
    factor = np.float32(math.sqrt(W) / G)
    cosine = np.cos(angle_tab) * factor
    sine_part = np.sin(angle_tab) * factor
    return np.stack([np.stack([cosine, -sine_part], 1), np.stack([sine_part, cosine], 1)], 0)


def kernel_tables():
    fwd = forward_table()
    inv = inverse_table()
    two = np.eye(2, dtype=np.float32)
    table_z = np.einsum("czdn,vw,ij->jviczdwn", fwd, two, two).reshape(2, 8 * W, 4 * G)
    back_z = np.einsum("dncz,vw,ij->jdwnvicz", inv, two, two).reshape(2, 4 * G, 8 * W)
    fwd_y = fwd.reshape(2, W // 2, 2, 2, G)
    table_y = np.einsum("dgpem->empdg", fwd_y).reshape(2 * G, 2 * W)
    table_x = np.einsum("dxem->emxd", fwd).reshape(2 * G, 2 * W)
    back_x = np.einsum("emdx->xdem", inv).reshape(2 * W, 2 * G)
    inv_y = inv.reshape(2, G, 2, W // 2, 2)
    back_y = np.einsum("dmcgp->pcgdm", inv_y).reshape(2 * W, 2 * G)
    listed = (table_z, table_y, table_x, back_x, back_y, back_z)
    return [jnp.asarray(t, dtype=jnp.bfloat16) for t in listed]


def kinetic_table():
    wave = np.arange(W, dtype=np.int32) - W // 2
    sq = wave * wave
    squared = sq[:, None, None, None] + sq[None, :, None, None] + sq[None, None, None, :]
    squared = np.broadcast_to(squared, (W, W, 2, W)).reshape(W * W // 2, 4 * W)
    return np.float32(kinetic_scale * 0.5) * squared.astype(np.float32)


def mm(left, right):
    return jnp.dot(left, right, preferred_element_type=jnp.float32)


def apply_kernel(
    vec_ref, pot_ref, kin_ref, tz_ref, ty_ref, tx_ref, bx_ref, by_ref, bz_ref,
    out_ref, ritz_ref, dens_ref, zs_ref, s_ref,
):
    lanes = 2 * G
    half = W // 2
    rows = W * half
    bf = jnp.bfloat16

    @pl.when(pl.program_id(0) == 0)
    def _():
        dens_ref[...] = jnp.zeros_like(dens_ref)

    def pair_in():
        return jnp.concatenate(
            [vec_ref[:, v].reshape(rows, 4 * W) for v in range(2)], axis=1
        )

    vecs = pair_in()
    for p in range(2):
        zs_ref[p] = mm(vecs, tz_ref[p]).astype(bf)

    def y_step(i, carry):
        cols = []
        for k in range(2):
            at = pl.ds(pl.multiple_of((2 * i + k) * half, half), half)
            parts = [zs_ref[p, at, d * lanes : (d + 1) * lanes] for p in range(2) for d in range(2)]
            cols.append(jnp.concatenate(parts, axis=0))
        done = mm(ty_ref[...], jnp.concatenate(cols, axis=1))
        for k in range(2):
            at = pl.ds(pl.multiple_of((2 * i + k) * lanes, lanes), lanes)
            s_ref[at, :] = done[:, k * lanes : (k + 1) * lanes]
        return carry

    lax.fori_loop(0, W // 2, y_step, 0, unroll=4)

    def x_step(i, carry):
        ats = [pl.ds(2 * i + k, 2 * W, stride=G) for k in range(2)]
        cols = [s_ref[at, :].astype(bf) for at in ats]
        done = mm(tx_ref[...], jnp.concatenate(cols, axis=1))
        real, imag = (done[:G], done[G:])
        pot = jnp.concatenate([pot_ref[2 * i], pot_ref[2 * i + 1]], axis=1)
        square = real * real + imag * imag
        for k in range(2):
            dens_ref[2 * i + k] += square[:, k * lanes : (k + 1) * lanes]
        weighted = jnp.concatenate([(real * pot).astype(bf), (imag * pot).astype(bf)], axis=0)
        back = mm(bx_ref[...], weighted)
        for k in range(2):
            s_ref[ats[k], :] = back[:, k * lanes : (k + 1) * lanes]
        return carry

    lax.fori_loop(0, G // 2, x_step, 0, unroll=4)

    def back_y_step(i, carry):
        cols = []
        for k in range(2):
            at = pl.ds(pl.multiple_of((2 * i + k) * lanes, lanes), lanes)
            cols.append(s_ref[at, :].astype(bf))
        done = mm(by_ref[...], jnp.concatenate(cols, axis=1)).astype(bf)
        for k in range(2):
            at = pl.ds(pl.multiple_of((2 * i + k) * half, half), half)
            for p in range(2):
                for c in range(2):
                    r = (2 * p + c) * half
                    zs_ref[p, at, c * lanes : (c + 1) * lanes] = done[
                        r : r + half, k * lanes : (k + 1) * lanes
                    ]
        return carry

    lax.fori_loop(0, W // 2, back_y_step, 0, unroll=4)

    local = mm(zs_ref[0], bz_ref[0]) + mm(zs_ref[1], bz_ref[1])
    kin = kin_ref[...]
    npw_total = W * W * W
    for v in range(2):
        orb = vec_ref[:, v].reshape(rows, 4 * W).astype(jnp.float32)
        ham = kin * orb + local[:, v * 4 * W : (v + 1) * 4 * W]
        numerator = jnp.sum(jnp.sum(orb * ham, axis=0, keepdims=True), axis=1, keepdims=True)
        denominator = jnp.sum(jnp.sum(orb * orb, axis=0, keepdims=True), axis=1, keepdims=True)
        ritz = numerator / npw_total / (denominator / npw_total + epsilon)
        search = ((ham - ritz * orb) / (1.0 + kin)).astype(bf)
        out_ref[:, v] = search.reshape(vec_ref.shape[0], *vec_ref.shape[2:])
        ritz_ref[0, :, v * 128 : (v + 1) * 128] = jnp.broadcast_to(ritz, (8, 128))


def apply_local(whole, potential):
    devices, vectors, planes, half, lanes = whole.shape
    tabs = kernel_tables()
    kin = jnp.asarray(kinetic_table())
    block = (devices, 2, planes, half, lanes)

    def fixed(arr):
        return pl.BlockSpec(arr.shape, lambda p, n=arr.ndim: (0,) * n)

    flops = vectors * 2 * 2 * (W * W * 2 * W * 2 * G + W * G * 2 * W * 2 * G + G * G * 2 * W * 2 * G)
    return pl.pallas_call(
        apply_kernel,
        grid=(vectors // 2,),
        in_specs=[pl.BlockSpec(block, lambda p: (0, p, 0, 0, 0)), fixed(potential), fixed(kin)]
        + [fixed(t) for t in tabs],
        out_specs=[
            pl.BlockSpec(block, lambda p: (0, p, 0, 0, 0)),
            pl.BlockSpec((1, 8, 256), lambda p: (p, 0, 0)),
            pl.BlockSpec((G, G, 2 * G), lambda p: (0, 0, 0)),
        ],
        out_shape=[
            jax.ShapeDtypeStruct(whole.shape, jnp.bfloat16),
            jax.ShapeDtypeStruct((vectors // 2, 8, 256), jnp.float32),
            jax.ShapeDtypeStruct((G, G, 2 * G), jnp.float32),
        ],
        scratch_shapes=[
            pltpu.VMEM((2, W * W // 2, 4 * G), jnp.bfloat16),
            pltpu.VMEM((W * 2 * G, 2 * G), jnp.float32),
        ],
        compiler_params=pltpu.CompilerParams(
            dimension_semantics=("arbitrary",), vmem_limit_bytes=48 * 1024 * 1024
        ),
        cost_estimate=pl.CostEstimate(flops=flops, bytes_accessed=8 << 20, transcendentals=0),
        name="apply_local",
    )(whole, potential, kin, *tabs)


def turn_kernel(c_ref, r_ref, out_ref):
    block = c_ref[...]
    out_ref[0] = block
    size = r_ref.shape[0]
    for t in range(block.shape[1] // size):
        at = slice(t * size, (t + 1) * size)
        out_ref[1, :, at] = mm(block[:, at], r_ref[...]).astype(jnp.bfloat16)


def with_turned(flat_all):
    bands, entries = flat_all.shape
    one = np.zeros((2, W, 2, W), np.float32)
    one[1, :, 0, :] = -np.eye(W)
    one[0, :, 1, :] = np.eye(W)
    turn = np.kron(np.eye(4, dtype=np.float32), one.reshape(2 * W, 2 * W))
    turn = jnp.asarray(turn, dtype=jnp.bfloat16)
    tile = 256
    return pl.pallas_call(
        turn_kernel,
        grid=(bands // tile,),
        in_specs=[
            pl.BlockSpec((tile, entries), lambda p: (p, 0)),
            pl.BlockSpec(turn.shape, lambda p: (0, 0)),
        ],
        out_specs=pl.BlockSpec((2, tile, entries), lambda p: (0, p, 0)),
        out_shape=jax.ShapeDtypeStruct((2, bands, entries), jnp.bfloat16),
        compiler_params=pltpu.CompilerParams(
            dimension_semantics=("arbitrary",), vmem_limit_bytes=40 * 1024 * 1024
        ),
        cost_estimate=pl.CostEstimate(
            flops=2 * bands * entries * 256, bytes_accessed=6 * bands * entries, transcendentals=0
        ),
        name="with_turned",
    )(flat_all, turn)


def wrap_offset(values):
    return jnp.mod(values + G // 2, G) - G // 2


def gaussians(coords, grid_cells):
    offset = wrap_offset(grid_cells[None, :] - coords[:, None]).astype(jnp.float32)
    return (jnp.exp(-offset * offset / (2.0 * sigma_cells * sigma_cells)), offset)


def atom_tables(own_pos, y_cells):
    grid_cells = jnp.arange(G, dtype=jnp.int32)
    gauss_x, offset_x = gaussians(own_pos[0], grid_cells)
    gauss_y, offset_y = gaussians(own_pos[1], y_cells)
    gauss_z, offset_z = gaussians(own_pos[2], grid_cells)
    return (gauss_x, offset_x, gauss_y, offset_y, gauss_z, offset_z)


def local_potential(tables, strength):
    gauss_x, offset_x, gauss_y, offset_y, gauss_z, offset_z = tables
    atom_count = gauss_x.shape[0]
    joined = (gauss_y[:, :, None] * gauss_z[:, None, :]).reshape(atom_count, -1)
    potential = jnp.dot((strength[:, None] * gauss_x).T, joined, precision=highest)
    return (potential, joined)


def atom_forces(density, tables, joined, strength):
    gauss_x, offset_x, gauss_y, offset_y, gauss_z, offset_z = tables
    atom_count = gauss_x.shape[0]
    with_y = ((gauss_y * offset_y)[:, :, None] * gauss_z[:, None, :]).reshape(atom_count, -1)
    with_z = (gauss_y[:, :, None] * (gauss_z * offset_z)[:, None, :]).reshape(atom_count, -1)
    stacked = jnp.concatenate([joined, with_y, with_z], 0)
    moments = jnp.dot(density, stacked.T, precision=highest)
    prefactor = -strength / (sigma_cells * sigma_cells)
    force_x = prefactor * jnp.sum(gauss_x * offset_x * moments[:, :atom_count].T, 1)
    force_y = prefactor * jnp.sum(gauss_x * moments[:, atom_count : 2 * atom_count].T, 1)
    force_z = prefactor * jnp.sum(gauss_x * moments[:, 2 * atom_count :].T, 1)
    return jnp.stack([force_x, force_y, force_z], 0)


def chain_forces(force, own_pos, before, after):
    ahead_step = wrap_offset(after - own_pos).astype(jnp.float32)
    behind = wrap_offset(own_pos - before).astype(jnp.float32)
    tangent_raw = ahead_step + behind
    entries = 3 * own_pos.shape[1]
    tangent = (
        tangent_raw * lax.rsqrt(jnp.mean(tangent_raw * tangent_raw) + epsilon) / math.sqrt(entries)
    )
    length_ahead = jnp.sqrt(entries * (jnp.mean(ahead_step * ahead_step) + epsilon))
    length_behind = jnp.sqrt(entries * (jnp.mean(behind * behind) + epsilon))
    along_path = jnp.sum(force * tangent)
    band_push = (
        force - along_path * tangent + spring_constant * (length_ahead - length_behind) * tangent
    )
    return (band_push, along_path)


def body(coefficients, rotation, positions, start_pos, end_pos, species, depth):
    axes = ("band", "pw")
    devices = lax.axis_size(axes)
    coeff_all = coefficients[0]
    planes = coeff_all.shape[1]
    flat_all = coeff_all.reshape(BANDS, -1)
    vectors = BLOCK // devices
    orbitals = jnp.einsum("ib,ik->bk", rotation[0], flat_all, preferred_element_type=jnp.float32)
    orbitals = orbitals.astype(jnp.bfloat16).reshape(BLOCK, planes * (W // 2), 4 * W)
    whole = lax.all_to_all(orbitals, axes, split_axis=0, concat_axis=0, tiled=True)
    whole = whole.reshape(devices, vectors, planes, W // 2, 4 * W)
    both = with_turned(flat_all)
    kind_ids = jnp.arange(SPECIES, dtype=jnp.int32)
    strength = jnp.sum(jnp.where(species[:, None] == kind_ids[None, :], depth[None, :], 0.0), 1)
    own_pos = positions[0]
    tables = atom_tables(own_pos, jnp.arange(G, dtype=jnp.int32))
    potential, joined = local_potential(tables, strength)
    potential = jnp.swapaxes(potential.reshape(G, G, G), 0, 1)
    potential = jnp.concatenate([potential, potential], 2)
    search, ritz, density = apply_local(whole, potential)
    search = search.reshape(BLOCK, planes * (W // 2), 4 * W)
    search = lax.all_to_all(search, axes, split_axis=0, concat_axis=0, tiled=True)
    search = search.reshape(BLOCK, -1)
    density = jnp.swapaxes(density[:, :, :G] + density[:, :, G:], 0, 1).reshape(G, G * G) / BLOCK
    force_part = atom_forces(density, tables, joined, strength)
    own_ritz = ritz[:, 0, ::128].reshape(vectors)
    ritz_part = lax.dynamic_update_slice(
        jnp.zeros((BLOCK,), jnp.float32), own_ritz, (lax.axis_index(axes) * vectors,)
    )
    summed = lax.psum(jnp.concatenate([force_part.reshape(-1), ritz_part]), axes)
    atom_force = summed[: force_part.size].reshape(force_part.shape)
    ritz_values = summed[force_part.size :]
    npw_total = W * W * W
    stacked = both.reshape(2 * BANDS, -1)
    partial = jnp.einsum("ik,jk->ij", stacked, search, preferred_element_type=jnp.float32)
    partial = (partial / npw_total).astype(jnp.bfloat16)
    arrived = lax.all_to_all(partial, axes, split_axis=0, concat_axis=0, tiled=True)
    arrived = arrived.reshape(devices, 2 * BANDS // devices, BLOCK).astype(jnp.float32)
    own_sum = jnp.sum(arrived, 0).astype(jnp.bfloat16)
    intersections = lax.all_gather(own_sum, axes, axis=0, tiled=True)
    projection = jnp.einsum(
        "ij,ik->jk", intersections, stacked, preferred_element_type=jnp.float32
    )
    correction = (search.astype(jnp.float32) - projection).astype(jnp.bfloat16)
    correction = correction.reshape(BLOCK, planes, W * 2 * W)
    image_idx = lax.axis_index("img")
    before = passed_along(own_pos, "img", 1)
    after = passed_along(own_pos, "img", -1)
    before = jnp.where(image_idx == 0, start_pos, before)
    after = jnp.where(image_idx == lax.axis_size("img") - 1, end_pos, after)
    band_push, along_path = chain_forces(atom_force, own_pos, before, after)
    return (correction[None], ritz_values[None], band_push[None], along_path[None])


def solution(mesh):
    in_specs = (
        P("img", None, ("band", "pw"), None),
        P("img", None, None),
        P("img", None, None),
        P(),
        P(),
        P(),
        P(),
    )
    out_specs = (
        P("img", None, ("band", "pw"), None),
        P("img", None),
        P("img", None, None),
        P("img"),
    )
    return jax.shard_map(body, mesh=mesh, in_specs=in_specs, out_specs=out_specs, check_vma=False)
```
